256 devices in a mesh: seq: 16 (over z_lo, y, core), wide: 16 (over x, z_hi).
Axes of the slice: x: 4, y: 4, z: 8 (z_hi: 4, z_lo: 2; z = z_hi * 2 + z_lo), core: 2. Of those that a mesh axis runs over, the one named last changes fastest.
Arguments:
- qkv_proj: bfloat16 [3, 2, 16384, 8192], P(None, None, ('seq', 'wide')), may hold values from -6 to 6
- conv_kernel: float32 [3, 4, 8192], replicated, may hold values from -3 to 3
- qk_gain: float32 [2, 16, 512], P(None, 'wide'), may hold values from 0.4 to 2.5
- fast_init: float32 [3, 16, 512, 512], P(None, 'wide'), may hold values from -0.25 to 0.25
- step_size: float32 [16], P('wide'), may hold values from 0.2 to 1
Outputs:
- fast_out: bfloat16 [2, 16384, 8192], P(None, 'seq', 'wide')
The draws below stay inside these ranges and needn't reach their ends.
All inputs are finite; a program needn't handle non-finite values.
Results may differ from the reference program's by a relative error of at most 0.004.
Values may be sent and summed in bfloat16 or wider, within the bound.
No kernel may reach another device: no remote copies, remote signals or barrier semaphores. Data moves between devices by JAX's collectives and lax.ppermute only.
A program may use at most 128 MiB of HBM per device.

```python
import math
import jax
import jax.numpy as jnp
from jax import lax

HEAD = 512
HEADS = 16
D = 8192
GROUPS = 2
KW = 4
GROUP = 16384


def block_levels(rng, dims, split, low, top_value):
    def one(axis_at, parts):
        heights = jax.random.uniform(jax.random.fold_in(jax.random.fold_in(rng, 6), axis_at), (parts,), jnp.float32, low / len(split), top_value / len(split))
        return jnp.repeat(jnp.exp(heights), dims[axis_at] // parts).reshape((-1,) + (1,) * (len(dims) - axis_at - 1))

    gain = one(*split[0])
    for cut in split[1:]:
        gain = gain * one(*cut)
    return gain


def scatter_about(stream_key, dims, spread, limit, shards=(), kind=jnp.bfloat16):
    gain = block_levels(stream_key, dims, shards, -0.22, 0.18) if shards else 1.0
    values = jax.random.normal(stream_key, dims, jnp.float32) * spread * gain
    return jnp.minimum(jnp.maximum(values, -limit), limit).astype(kind)


def setup_inputs(seed: int = 0) -> dict:
    arg_keys = jax.random.split(jax.random.key(seed), 6)
    return {
        "qkv_proj": scatter_about(arg_keys[0], (3, GROUPS, GROUP, D), 1.0, 6.0, ((2, 256),)),
        "conv_kernel": scatter_about(arg_keys[1], (3, KW, D), 0.5, 3.0, (), jnp.float32),
        "qk_gain": jnp.clip(jnp.exp(math.log(2.5) - 1.8325814 * jax.random.uniform(arg_keys[2], (2, HEADS, HEAD), jnp.float32) ** block_levels(arg_keys[2], (2, HEADS, HEAD), ((1, 16),), -0.2, 0.2)), 0.4, 2.5),
        "fast_init": scatter_about(arg_keys[3], (3, HEADS, HEAD, HEAD), HEAD ** -0.5, 0.25, ((1, 16),), jnp.float32),
        "step_size": jnp.clip(jnp.exp(math.log(1.0) - 1.609438 * jax.random.uniform(arg_keys[4], (HEADS,), jnp.float32) ** block_levels(arg_keys[4], (HEADS,), ((0, 16),), -0.2, 0.2)), 0.2, 1.0),
    }


EPS = 1e-06
BETA = 0.6

def matmul(left, right):
    return jnp.dot(left, right, preferred_element_type=jnp.float32)

def contract_rows(left, right):
    return lax.dot_general(left, right, (((0,), (0,)), ((), ())), preferred_element_type=jnp.float32)

def contract_cols(left, right):
    return lax.dot_general(left, right, (((1,), (1,)), ((), ())), preferred_element_type=jnp.float32)

def rms_rows(values_in):
    values_in = values_in.astype(jnp.float32)
    return values_in * lax.rsqrt(lax.optimization_barrier(jnp.mean(values_in * values_in, axis=-1, keepdims=True)) + EPS)

def normalize_columns(moment):
    return moment * lax.rsqrt(lax.optimization_barrier(jnp.mean(moment * moment, axis=1, keepdims=True)) + EPS)

def local_gradients(weights, keys_in, values_in):
    narrow = weights.astype(jnp.bfloat16)
    gate_pre = matmul(keys_in, narrow[0])
    up_pre = matmul(keys_in, narrow[1])
    sigmoid_gate = jax.nn.sigmoid(gate_pre)
    gate_act = gate_pre * sigmoid_gate
    hidden = (gate_act * up_pre).astype(jnp.bfloat16)
    back_hidden = contract_cols(values_in, narrow[2])
    g_down = contract_rows(hidden, values_in)
    err_gate = (back_hidden * up_pre * sigmoid_gate * (1.0 + gate_pre * (1.0 - sigmoid_gate))).astype(jnp.bfloat16)
    err_up = (back_hidden * gate_act).astype(jnp.bfloat16)
    g_gate = contract_rows(keys_in, err_gate)
    g_up = contract_rows(keys_in, err_up)
    return jnp.stack([g_gate, g_up, g_down])

def apply_fast(weights, queries):
    narrow = weights.astype(jnp.bfloat16)
    hidden = (jax.nn.silu(matmul(queries, narrow[0])) * matmul(queries, narrow[1])).astype(jnp.bfloat16)
    return matmul(hidden, narrow[2])

def reference(qkv_proj, conv_kernel, qk_gain, fast_init, step_size):

    def conv_one(stream_pair):
        stream, kernel = stream_pair
        flat_rows = stream.reshape(GROUPS * GROUP, D)
        padded = jnp.concatenate([jnp.zeros((KW - 1, D), flat_rows.dtype), flat_rows], axis=0)
        summed = jnp.zeros((GROUPS * GROUP, D), jnp.float32)
        for tap_index in range(KW):
            begin = KW - 1 - tap_index
            summed = summed + kernel[tap_index] * padded[begin:begin + GROUPS * GROUP].astype(jnp.float32)
        return jax.nn.silu(summed).astype(jnp.bfloat16).reshape(GROUPS, GROUP, D)
    activated = lax.map(conv_one, (qkv_proj, conv_kernel))

    def one_head(inputs_tuple):
        head_index, gains, weights, learn_rate = inputs_tuple
        group_data = lax.dynamic_slice_in_dim(activated, head_index * HEAD, HEAD, 3)
        step_scale = learn_rate * HEAD ** (-0.5)
        momentum = jnp.zeros_like(weights)
        outputs = []
        for group_index in range(GROUPS):
            queries = (rms_rows(group_data[0, group_index]) * gains[0]).astype(jnp.bfloat16)
            keys_in = (rms_rows(group_data[1, group_index]) * gains[1]).astype(jnp.bfloat16)
            values_in = group_data[2, group_index] * (-1.0 / GROUP)
            gradients = local_gradients(weights, keys_in, values_in)
            momentum = BETA * momentum + gradients
            weights = weights - step_scale * normalize_columns(momentum)
            outputs.append(apply_fast(weights, queries))
        return jnp.stack(outputs)
    per_head = lax.map(one_head, (jnp.arange(HEADS, dtype=jnp.int32), jnp.transpose(qk_gain, (1, 0, 2)), jnp.transpose(fast_init, (1, 0, 2, 3)), step_size))
    return jnp.transpose(per_head, (1, 2, 0, 3)).reshape(GROUPS, GROUP, D).astype(jnp.bfloat16)
```

```python
import jax
import jax.numpy as jnp
from jax import lax
from jax.experimental import pallas as pl
from jax.experimental.pallas import tpu as pltpu
from jax.sharding import PartitionSpec as P


HEAD = 512
GROUPS = 2
KW = 4
EPS = 1e-06
BETA = 0.6
ROWS = 1024
CHUNK = 256
BLOCKS = ROWS // CHUNK
LEAD = CHUNK // 64
BF = jnp.bfloat16
F32 = jnp.float32


def vmem():
    return pl.BlockSpec(memory_space=pltpu.VMEM)


def anywhere():
    return pl.BlockSpec(memory_space=pl.ANY)


def call(body, outs, ins, scratch=(), flops=0, nbytes=1 << 18, out_specs=None, limit=16, **more):
    return pl.pallas_call(
        body,
        out_shape=outs,
        in_specs=ins,
        out_specs=jax.tree.map(lambda _: vmem(), outs) if out_specs is None else out_specs,
        scratch_shapes=list(scratch),
        cost_estimate=pl.CostEstimate(flops=flops, bytes_accessed=nbytes, transcendentals=0),
        compiler_params=pltpu.CompilerParams(vmem_limit_bytes=limit << 20),
        **more,
    )


def sds(shape, dtype):
    return jax.ShapeDtypeStruct(shape, dtype)


def sigmoid(x):
    return 0.5 * jnp.tanh(0.5 * x) + 0.5


def conv_silu(current, previous, taps):
    extended = jnp.concatenate([previous, current], axis=0)
    total = taps[0:1] * current
    for j in range(1, KW):
        total = total + taps[j : j + 1] * pltpu.roll(extended, j, 0)[8:]
    return (total * sigmoid(total)).astype(BF)


def rms_scaled(act, gain):
    wide = act.astype(F32)
    scale = lax.rsqrt(jnp.mean(wide * wide, axis=-1, keepdims=True) + EPS)
    return (wide * scale * gain).astype(BF)


def nt(left, right):
    return lax.dot_general(left, right, (((1,), (1,)), ((), ())), preferred_element_type=F32)


def nn(left, right):
    return jnp.dot(left, right, preferred_element_type=F32)


def tn(left, right):
    return lax.dot_general(left, right, (((0,), (0,)), ((), ())), preferred_element_type=F32)


def own_taps(taps, stream):
    cols = pl.ds(pl.multiple_of(lax.axis_index("wide") * HEAD, HEAD), HEAD)
    return taps[stream, :, cols]


def edge_rows(first, tails, earlier, stream):
    later = lax.axis_index("seq") > 0
    here = tails[stream].astype(F32)
    if first:
        return jnp.where(later, here, jnp.zeros_like(here))
    return jnp.where(later, here, earlier[stream].astype(F32))


def conv_chunk(raw, stream, n, edge, taps):
    current = raw[pl.ds(LEAD * n, LEAD), stream].reshape(CHUNK, HEAD).astype(F32)
    inner = raw[jnp.maximum(LEAD * n - 1, 0), stream, 48:64, :].astype(F32)[8:]
    return conv_silu(current, jnp.where(n == 0, edge, inner), taps)


def chunk_rows(n):
    return pl.ds(pl.multiple_of(n * CHUNK, CHUNK), CHUNK)


def hbm():
    return pl.BlockSpec(memory_space=pltpu.HBM)


def spread_of(first_stream, streams, group):
    def body(source, out, stage, sems_in, sems_out):
        def pull(s, h):
            cols = pl.ds(h * HEAD, HEAD)
            spot = source.at[first_stream + s, group, :, cols]
            return pltpu.make_async_copy(spot, stage.at[s, h], sems_in.at[s, h])

        def push(s, h):
            return pltpu.make_async_copy(stage.at[s, h], out.at[h, s], sems_out.at[s, h])

        spots = [(s, h) for s in range(streams) for h in range(16)]
        for spot in spots:
            pull(*spot).start()
        for spot in spots:
            pull(*spot).wait()
            push(*spot).start()
        for spot in spots:
            push(*spot).wait()

    return call(
        body,
        sds((16, streams, 64, HEAD), BF),
        [hbm()],
        [
            pltpu.VMEM((streams, 16, 64, HEAD), BF),
            pltpu.SemaphoreType.DMA((streams, 16)),
            pltpu.SemaphoreType.DMA((streams, 16)),
        ],
        nbytes=streams << 21,
        out_specs=hbm(),
    )


def prepare(first, raw, tails, earlier, taps, gain):
    def body(raw, tails, earlier, taps, gain, keys, values):
        key_taps, value_taps = own_taps(taps, 1), own_taps(taps, 2)
        key_edge = edge_rows(first, tails, earlier, 0)
        value_edge = edge_rows(first, tails, earlier, 1)

        def step(n, carry):
            rows = chunk_rows(n)
            keys[rows, :] = rms_scaled(conv_chunk(raw, 0, n, key_edge, key_taps), gain[1])
            act = conv_chunk(raw, 1, n, value_edge, value_taps)
            values[rows, :] = (act.astype(F32) * (-1.0 / 16384)).astype(BF)
            return carry

        lax.fori_loop(0, BLOCKS, step, 0)

    rows = sds((ROWS, HEAD), BF)
    return call(body, [rows, rows], [vmem()] * 5, nbytes=8 << 20)(raw, tails, earlier, taps, gain)


def prepare_queries(first, raw, tails, earlier, taps, gain):
    def body(raw, tails, earlier, taps, gain, queries):
        query_taps = own_taps(taps, 0)
        edge = edge_rows(first, tails, earlier, 0)

        def step(n, carry):
            queries[chunk_rows(n), :] = rms_scaled(conv_chunk(raw, 0, n, edge, query_taps), gain[0])
            return carry

        lax.fori_loop(0, BLOCKS, step, 0)

    return call(body, sds((ROWS, HEAD), BF), [vmem()] * 5, nbytes=4 << 20)(
        raw, tails, earlier, taps, gain
    )


def gradients(keys, values, weights, plain):
    def body(keys, values, weights, keep, send, hs, gs, us):
        core = lax.axis_index("seq") & 1
        wg, wu, wd = (weights[m].astype(BF) for m in range(3))

        def step(n, carry):
            rows = chunk_rows(n)
            k = keys[rows, :]
            v = values[rows, :]
            if plain:
                a, b, back = nn(k, wg), nn(k, wu), nt(v, wd)
            else:
                a, b, back = nt(k, wg), nt(k, wu), nn(v, wd)
            sg = sigmoid(a)
            act = a * sg
            hs[rows, :] = (act * b).astype(BF)
            gs[rows, :] = (back * b * sg * (1.0 + a * (1.0 - sg))).astype(BF)
            us[rows, :] = (back * act).astype(BF)
            return carry

        lax.fori_loop(0, BLOCKS, step, 0)
        for half, out in ((1, send), (0, keep)):
            side = jnp.bitwise_xor(core, half)

            def block(n, carry, out=out, side=side):
                cols = pl.ds(pl.multiple_of(side * 256 + n * 128, 128), 128)
                for m, (left, right) in enumerate(((gs, keys), (us, keys), (values, hs))):
                    part = tn(left[:, cols], right[...]).astype(BF)
                    for q in range(2):
                        out[2 * n + q, m] = part[64 * q : 64 * q + 64]
                return carry

            lax.fori_loop(0, 2, block, 0)

    half = sds((4, 3, 64, HEAD), BF)
    return call(
        body,
        [half, half],
        [vmem()] * 3,
        [pltpu.VMEM((ROWS, HEAD), BF)] * 3,
        flops=6 * 2 * ROWS * HEAD * HEAD,
        nbytes=4 << 20,
        limit=24,
    )(keys, values, weights)


def pair_sum(keep, recv):
    def body(keep, recv, own, *sends):
        y = lax.axis_index("seq") >> 1 & 3
        own[...] = keep[y].astype(F32) + recv[y].astype(F32)
        for d, out in enumerate(sends):
            other = y + (d + 1) & 3
            out[...] = (keep[other].astype(F32) + recv[other].astype(F32)).astype(BF)

    block = (3, 64, HEAD)
    return call(body, [sds(block, F32)] + [sds(block, BF)] * 3, [vmem()] * 2)(keep, recv)


def ring_sum(own, parts):
    def body(own, one, two, three, out):
        out[...] = (own[...] + one[...].astype(F32) + two[...].astype(F32) + three[...].astype(F32)).astype(BF)

    return call(body, sds((3, 64, HEAD), BF), [vmem()] * 4)(own, *parts)


def update(scale, mine, recv, weights, moment):
    fresh = moment is None

    def body(scale, mine, recv, weights, *rest):
        grad = mine[...].astype(F32) + recv[...].astype(F32)
        if fresh:
            mom = grad
        else:
            mom = BETA * rest[0][...] + grad
        moment_out, weights_out, narrow = rest[-3:]
        norm = lax.rsqrt(jnp.mean(mom * mom, axis=-1, keepdims=True) + EPS)
        new = weights[...] - (scale[0] * HEAD ** (-0.5)) * (mom * norm)
        moment_out[...] = mom
        weights_out[...] = new
        narrow[...] = new.astype(BF)

    block = (3, 64, HEAD)
    ins = [scale, mine, recv, weights] + ([] if fresh else [moment])
    return call(
        body,
        [sds(block, F32), sds(block, F32), sds(block, BF)],
        [pl.BlockSpec(memory_space=pltpu.SMEM)] + [vmem()] * (len(ins) - 1),
    )(*ins)


def assemble(pieces):
    def body(*refs):
        out = refs[8]
        seq = lax.axis_index("seq")
        core, y = seq & 1, seq >> 1 & 3
        for k, piece in enumerate(refs[:8]):
            side = jnp.bitwise_xor(core, k // 4)
            spot = y + 4 - k % 4 & 3
            rows = pl.ds(pl.multiple_of(side * 256 + spot * 64, 64), 64)
            for m in range(3):
                out[m, rows, :] = piece[m]

    return call(body, sds((3, HEAD, HEAD), BF), [vmem()] * 8)(*pieces)


def apply_fast(queries, weights, group, earlier):
    def body(queries, weights, *rest):
        out, stage, sems = rest[-3:]

        def copy(n):
            rows = chunk_rows(n)
            return pltpu.make_async_copy(stage.at[rows], out.at[group, rows], sems.at[n])

        def step(n, carry):
            rows = chunk_rows(n)
            q = queries[rows, :]
            a = nt(q, weights[0])
            b = nt(q, weights[1])
            hidden = (a * sigmoid(a) * b).astype(BF)
            stage[rows, :] = nt(hidden, weights[2]).astype(BF)
            copy(n).start()
            return carry

        lax.fori_loop(0, BLOCKS, step, 0)
        for n in range(BLOCKS):
            copy(n).wait()

    more = [] if earlier is None else [earlier]
    return call(
        body,
        sds((GROUPS, ROWS, HEAD), BF),
        [vmem()] * 2 + [anywhere()] * len(more),
        [pltpu.VMEM((ROWS, HEAD), BF), pltpu.SemaphoreType.DMA((BLOCKS,))],
        flops=3 * 2 * ROWS * HEAD * HEAD,
        nbytes=4 << 20,
        out_specs=anywhere(),
        input_output_aliases={2: 0} if more else {},
    )(queries, weights, *more)


def seq_permute(value, target):
    return lax.ppermute(value, "seq", [(i, target(i)) for i in range(16)])


def core_swap(value):
    return seq_permute(value, lambda i: i ^ 1)


def z_swap(value):
    return seq_permute(value, lambda i: i ^ 8)


def y_shift(value, d):
    return seq_permute(value, lambda i: (i & 9) | (((i >> 1 & 3) + d & 3) << 1))


def regroup(qkv_proj, first_stream, streams, group):
    spread = spread_of(first_stream, streams, group)(qkv_proj)
    return lax.all_to_all(spread, "wide", 0, 0, tiled=True)


def tails_behind(raw):
    return seq_permute(raw[15, :, 56:64, :], lambda i: (i + 1) % 16)


def reduce_pieces(keep, send):
    recv = core_swap(send)
    own, *sends = pair_sum(keep, recv)
    parts = [y_shift(s, d + 1) for d, s in enumerate(sends)]
    mine = ring_sum(own, parts)
    return mine, z_swap(mine)


def gather_pieces(narrow):
    pieces = [narrow] + [y_shift(narrow, d) for d in (1, 2, 3)]
    return pieces + [core_swap(p) for p in pieces]


def local(qkv_proj, conv_kernel, qk_gain, fast_init, step_size):
    return program(qkv_proj, conv_kernel, qk_gain, fast_init[:, 0], step_size)


def program(qkv_proj, conv_kernel, qk_gain, start, step_size):
    seq = lax.axis_index("seq")
    own_at = (seq & 1) * 256 + (seq >> 1 & 3) * 64
    state = jnp.swapaxes(lax.dynamic_slice_in_dim(start, own_at, 64, 2), 1, 2)

    kv0 = regroup(qkv_proj, 1, 2, 0)
    tails0 = tails_behind(kv0)
    kv1 = regroup(qkv_proj, 1, 2, 1)
    tails1 = tails_behind(kv1)
    q0 = regroup(qkv_proj, 0, 1, 0)
    qtails0 = tails_behind(q0)
    q1 = regroup(qkv_proj, 0, 1, 1)
    qtails1 = tails_behind(q1)

    keys, values = prepare(True, kv0, tails0, tails0, conv_kernel, qk_gain)
    mine, recv = reduce_pieces(*gradients(keys, values, start, True))
    moment, state, narrow = update(step_size, mine, recv, state, None)
    weights1 = assemble(gather_pieces(narrow))
    keys, values = prepare(False, kv1, tails1, tails0, conv_kernel, qk_gain)
    mine, recv = reduce_pieces(*gradients(keys, values, weights1, False))
    moment, state, narrow = update(step_size, mine, recv, state, moment)
    weights2 = assemble(gather_pieces(narrow))
    queries0 = prepare_queries(True, q0, qtails0, qtails0, conv_kernel, qk_gain)
    out = apply_fast(queries0, weights1, 0, None)
    queries1 = prepare_queries(False, q1, qtails1, qtails0, conv_kernel, qk_gain)
    return apply_fast(queries1, weights2, 1, out)


def solution(mesh):
    in_specs = (
        P(None, None, ("seq", "wide"), None),
        P(),
        P(None, "wide", None),
        P(None, "wide", None, None),
        P("wide"),
    )
    out_specs = P(None, "seq", "wide")
    return jax.shard_map(local, mesh=mesh, in_specs=in_specs, out_specs=out_specs, check_vma=False)
```

```python
import jax
import jax.numpy as jnp
from jax import lax
from jax.experimental import pallas as pl
from jax.experimental.pallas import tpu as pltpu
from jax.sharding import PartitionSpec as P


HEAD = 512
GROUPS = 2
KW = 4
EPS = 1e-06
BETA = 0.6
ROWS = 1024
CHUNK = 256
BLOCKS = ROWS // CHUNK
LEAD = CHUNK // 64
BF = jnp.bfloat16
F32 = jnp.float32


def vmem():
    return pl.BlockSpec(memory_space=pltpu.VMEM)


def anywhere():
    return pl.BlockSpec(memory_space=pl.ANY)


def call(body, outs, ins, scratch=(), flops=0, nbytes=1 << 18, out_specs=None, limit=16, **more):
    return pl.pallas_call(
        body,
        out_shape=outs,
        in_specs=ins,
        out_specs=jax.tree.map(lambda _: vmem(), outs) if out_specs is None else out_specs,
        scratch_shapes=list(scratch),
        cost_estimate=pl.CostEstimate(flops=flops, bytes_accessed=nbytes, transcendentals=0),
        compiler_params=pltpu.CompilerParams(vmem_limit_bytes=limit << 20),
        **more,
    )


def sds(shape, dtype):
    return jax.ShapeDtypeStruct(shape, dtype)


def sigmoid(x):
    return 0.5 * jnp.tanh(0.5 * x) + 0.5


def conv_silu(current, previous, taps):
    extended = jnp.concatenate([previous, current], axis=0)
    total = taps[0:1] * current
    for j in range(1, KW):
        total = total + taps[j : j + 1] * pltpu.roll(extended, j, 0)[8:]
    return (total * sigmoid(total)).astype(BF)


def rms_scaled(act, gain):
    wide = act.astype(F32)
    scale = lax.rsqrt(jnp.mean(wide * wide, axis=-1, keepdims=True) + EPS)
    return (wide * scale * gain).astype(BF)


def nt(left, right):
    return lax.dot_general(left, right, (((1,), (1,)), ((), ())), preferred_element_type=F32)


def nn(left, right):
    return jnp.dot(left, right, preferred_element_type=F32)


def tn(left, right):
    return lax.dot_general(left, right, (((0,), (0,)), ((), ())), preferred_element_type=F32)


def own_taps(taps, stream):
    cols = pl.ds(pl.multiple_of(lax.axis_index("wide") * HEAD, HEAD), HEAD)
    return taps[stream, :, cols]


def edge_rows(first, tails, earlier, stream):
    later = lax.axis_index("seq") > 0
    here = tails[stream].astype(F32)
    if first:
        return jnp.where(later, here, jnp.zeros_like(here))
    return jnp.where(later, here, earlier[stream].astype(F32))


def conv_chunk(raw, stream, n, edge, taps):
    current = raw[stream, pl.ds(LEAD * n, LEAD)].reshape(CHUNK, HEAD).astype(F32)
    inner = raw[stream, jnp.maximum(LEAD * n - 1, 0), 48:64, :].astype(F32)[8:]
    return conv_silu(current, jnp.where(n == 0, edge, inner), taps)


def raw_copy(source, raw, sems, offset, stream, n):
    lead = pl.ds(LEAD * n, LEAD)
    return pltpu.make_async_copy(
        source.at[lead, offset + stream], raw.at[stream, lead], sems.at[stream, n]
    )


def raw_scratch(streams):
    return [pltpu.VMEM((streams, 16, 64, HEAD), BF), pltpu.SemaphoreType.DMA((streams, BLOCKS))]


def chunk_rows(n):
    return pl.ds(pl.multiple_of(n * CHUNK, CHUNK), CHUNK)


def hbm():
    return pl.BlockSpec(memory_space=pltpu.HBM)


def in_hbm(value):
    return pltpu.with_memory_space_constraint(value, pltpu.HBM)


def spread(source, spots):
    def body(source, out, stage, sems_in, sems_out):
        def pull(s, h):
            stream, group = spots[s]
            cols = pl.ds(h * HEAD, HEAD)
            return pltpu.make_async_copy(
                source.at[stream, group, :, cols], stage.at[h, s], sems_in.at[s, h]
            )

        def push(s, h):
            return pltpu.make_async_copy(stage.at[h, s], out.at[h, s], sems_out.at[s, h])

        both = [(s, h) for s in range(2) for h in range(16)]
        for spot in both:
            pull(*spot).start()
        for spot in both:
            pull(*spot).wait()
            push(*spot).start()
        for spot in both:
            push(*spot).wait()

    return call(
        body,
        sds((16, 2, 64, HEAD), BF),
        [hbm()],
        [
            pltpu.VMEM((16, 2, 64, HEAD), BF),
            pltpu.SemaphoreType.DMA((2, 16)),
            pltpu.SemaphoreType.DMA((2, 16)),
        ],
        nbytes=4 << 20,
        out_specs=hbm(),
        limit=60,
    )(in_hbm(source))


def prepare(first, source, tails, earlier, taps, gain, start):
    def body(source, tails, earlier, taps, gain, *rest):
        if first:
            start, keys, values, narrow, raw, sems, wide, wide_sem = rest
        else:
            keys, values, raw, sems = rest
        for n in range(BLOCKS):
            for stream in range(2):
                raw_copy(source, raw, sems, 0, stream, n).start()
        if first:
            fetch = pltpu.make_async_copy(start, wide, wide_sem)
            fetch.start()
        key_taps, value_taps = own_taps(taps, 1), own_taps(taps, 2)
        key_edge = edge_rows(first, tails, earlier, 0)
        value_edge = edge_rows(first, tails, earlier, 1)

        def step(n, carry):
            rows = chunk_rows(n)
            raw_copy(source, raw, sems, 0, 0, n).wait()
            raw_copy(source, raw, sems, 0, 1, n).wait()
            keys[rows, :] = rms_scaled(conv_chunk(raw, 0, n, key_edge, key_taps), gain[1])
            act = conv_chunk(raw, 1, n, value_edge, value_taps)
            values[rows, :] = (act.astype(F32) * (-1.0 / 16384)).astype(BF)
            return carry

        lax.fori_loop(0, BLOCKS, step, 0)
        if first:
            fetch.wait()
            narrow[...] = wide[...].astype(BF)

    rows = sds((ROWS, HEAD), BF)
    square = (3, HEAD, HEAD)
    outs = [rows, rows] + ([sds(square, BF)] if first else [])
    scratch = raw_scratch(2) + ([pltpu.VMEM(square, F32), pltpu.SemaphoreType.DMA(())] if first else [])
    ins = [in_hbm(source), tails, earlier, taps, gain] + ([in_hbm(start)] if first else [])
    specs = [hbm()] + [vmem()] * 4 + ([hbm()] if first else [])
    return call(body, outs, specs, scratch, nbytes=8 << 20, limit=24)(*ins)


def prepare_queries(source, tails, taps, gain):
    def body(source, tails, taps, gain, *rest):
        raw, sems = rest[-2:]
        for group in range(GROUPS):
            for n in range(BLOCKS):
                raw_copy(source, raw, sems, 0, group, n).start()
        query_taps = own_taps(taps, 0)
        for group, queries in enumerate(rest[:GROUPS]):
            edge = edge_rows(group == 0, tails.at[group : group + 1], tails, 0)

            def step(n, carry, group=group, queries=queries, edge=edge):
                raw_copy(source, raw, sems, 0, group, n).wait()
                act = conv_chunk(raw, group, n, edge, query_taps)
                queries[chunk_rows(n), :] = rms_scaled(act, gain[0])
                return carry

            lax.fori_loop(0, BLOCKS, step, 0)

    rows = sds((ROWS, HEAD), BF)
    return call(
        body, [rows, rows], [hbm()] + [vmem()] * 3, raw_scratch(GROUPS), nbytes=8 << 20
    )(in_hbm(source), tails, taps, gain)


def gradients(keys, values, weights, plain):
    def body(keys, values, weights, keep, send, hs, gs, us):
        core = lax.axis_index("seq") & 1
        wg, wu, wd = (weights[m].astype(BF) for m in range(3))

        def step(n, carry):
            rows = chunk_rows(n)
            k = keys[rows, :]
            v = values[rows, :]
            if plain:
                a, b, back = nn(k, wg), nn(k, wu), nt(v, wd)
            else:
                a, b, back = nt(k, wg), nt(k, wu), nn(v, wd)
            sg = sigmoid(a)
            act = a * sg
            hs[rows, :] = (act * b).astype(BF)
            gs[rows, :] = (back * b * sg * (1.0 + a * (1.0 - sg))).astype(BF)
            us[rows, :] = (back * act).astype(BF)
            return carry

        lax.fori_loop(0, BLOCKS, step, 0)
        for half, out in ((1, send), (0, keep)):
            side = jnp.bitwise_xor(core, half)

            def block(n, carry, out=out, side=side):
                cols = pl.ds(pl.multiple_of(side * 256 + n * 128, 128), 128)
                for m, (left, right) in enumerate(((gs, keys), (us, keys), (values, hs))):
                    part = tn(left[:, cols], right[...]).astype(BF)
                    for q in range(2):
                        out[2 * n + q, m] = part[64 * q : 64 * q + 64]
                return carry

            lax.fori_loop(0, 2, block, 0)

    half = sds((4, 3, 64, HEAD), BF)
    return call(
        body,
        [half, half],
        [vmem()] * 3,
        [pltpu.VMEM((ROWS, HEAD), BF)] * 3,
        flops=6 * 2 * ROWS * HEAD * HEAD,
        nbytes=4 << 20,
        limit=24,
    )(keys, values, weights)


def pair_sum(keep, recv):
    def body(keep, recv, own, *sends):
        y = lax.axis_index("seq") >> 1 & 3
        own[...] = keep[y].astype(F32) + recv[y].astype(F32)
        for d, out in enumerate(sends):
            other = y + (d + 1) & 3
            out[...] = (keep[other].astype(F32) + recv[other].astype(F32)).astype(BF)

    block = (3, 64, HEAD)
    return call(body, [sds(block, F32)] + [sds(block, BF)] * 3, [vmem()] * 2)(keep, recv)


def ring_sum(own, parts):
    def body(own, one, two, three, out):
        out[...] = (own[...] + one[...].astype(F32) + two[...].astype(F32) + three[...].astype(F32)).astype(BF)

    return call(body, sds((3, 64, HEAD), BF), [vmem()] * 4)(own, *parts)


def update(scale, mine, recv, weights, moment):
    fresh = moment is None

    def body(scale, mine, recv, weights, *rest):
        grad = mine[...].astype(F32) + recv[...].astype(F32)
        if fresh:
            mom = grad
        else:
            mom = BETA * rest[0][...] + grad
        moment_out, weights_out, narrow = rest[-3:]
        norm = lax.rsqrt(jnp.mean(mom * mom, axis=-1, keepdims=True) + EPS)
        new = weights[...] - (scale[0] * HEAD ** (-0.5)) * (mom * norm)
        moment_out[...] = mom
        weights_out[...] = new
        narrow[...] = new.astype(BF)

    block = (3, 64, HEAD)
    ins = [scale, mine, recv, weights] + ([] if fresh else [moment])
    return call(
        body,
        [sds(block, F32), sds(block, F32), sds(block, BF)],
        [pl.BlockSpec(memory_space=pltpu.SMEM)] + [vmem()] * (len(ins) - 1),
    )(*ins)


def assemble(pieces):
    def body(*refs):
        out = refs[8]
        seq = lax.axis_index("seq")
        core, y = seq & 1, seq >> 1 & 3
        for k, piece in enumerate(refs[:8]):
            side = jnp.bitwise_xor(core, k // 4)
            spot = y + 4 - k % 4 & 3
            rows = pl.ds(pl.multiple_of(side * 256 + spot * 64, 64), 64)
            for m in range(3):
                out[m, rows, :] = piece[m]

    return call(body, sds((3, HEAD, HEAD), BF), [vmem()] * 8)(*pieces)


def apply_fast(queries, weights, group, earlier):
    def body(queries, weights, *rest):
        out, stage, sems = rest[-3:]

        def copy(n):
            rows = chunk_rows(n)
            return pltpu.make_async_copy(stage.at[rows], out.at[group, rows], sems.at[n])

        def step(n, carry):
            rows = chunk_rows(n)
            q = queries[rows, :]
            a = nt(q, weights[0])
            b = nt(q, weights[1])
            hidden = (a * sigmoid(a) * b).astype(BF)
            stage[rows, :] = nt(hidden, weights[2]).astype(BF)
            copy(n).start()
            return carry

        lax.fori_loop(0, BLOCKS, step, 0)
        for n in range(BLOCKS):
            copy(n).wait()

    more = [] if earlier is None else [earlier]
    return call(
        body,
        sds((GROUPS, ROWS, HEAD), BF),
        [vmem()] * 2 + [anywhere()] * len(more),
        [pltpu.VMEM((ROWS, HEAD), BF), pltpu.SemaphoreType.DMA((BLOCKS,))],
        flops=3 * 2 * ROWS * HEAD * HEAD,
        nbytes=4 << 20,
        out_specs=anywhere(),
        input_output_aliases={2: 0} if more else {},
    )(queries, weights, *more)


def seq_permute(value, target):
    return lax.ppermute(value, "seq", [(i, target(i)) for i in range(16)])


def core_swap(value):
    return seq_permute(value, lambda i: i ^ 1)


def z_swap(value):
    return seq_permute(value, lambda i: i ^ 8)


def y_shift(value, d):
    return seq_permute(value, lambda i: (i & 9) | (((i >> 1 & 3) + d & 3) << 1))


def regroup(qkv_proj, spots):
    ready = spread(qkv_proj, spots)
    return lax.all_to_all(ready, "wide", 0, 0, tiled=True)


def tails_behind(raw):
    return seq_permute(raw[15, :, 56:64, :], lambda i: (i + 1) % 16)


def reduce_pieces(keep, send):
    recv = core_swap(send)
    own, *sends = pair_sum(keep, recv)
    parts = [y_shift(s, d + 1) for d, s in enumerate(sends)]
    mine = ring_sum(own, parts)
    return mine, z_swap(mine)


def gather_pieces(narrow):
    pieces = [narrow] + [y_shift(narrow, d) for d in (1, 2, 3)]
    return pieces + [core_swap(p) for p in pieces]


def local(qkv_proj, conv_kernel, qk_gain, fast_init, step_size):
    return program(qkv_proj, conv_kernel, qk_gain, fast_init[:, 0], step_size)


def program(qkv_proj, conv_kernel, qk_gain, start, step_size):
    seq = lax.axis_index("seq")
    own_at = (seq & 1) * 256 + (seq >> 1 & 3) * 64
    state = jnp.swapaxes(lax.dynamic_slice_in_dim(start, own_at, 64, 2), 1, 2)

    kv0 = regroup(qkv_proj, ((1, 0), (2, 0)))
    tails0 = tails_behind(kv0)
    kv1 = regroup(qkv_proj, ((1, 1), (2, 1)))
    tails1 = tails_behind(kv1)
    q = regroup(qkv_proj, ((0, 0), (0, 1)))
    qtails = tails_behind(q)

    keys, values, narrow = prepare(True, kv0, tails0, tails0, conv_kernel, qk_gain, start)
    mine, recv = reduce_pieces(*gradients(keys, values, narrow, True))
    moment, state, narrow = update(step_size, mine, recv, state, None)
    weights1 = assemble(gather_pieces(narrow))
    keys, values = prepare(False, kv1, tails1, tails0, conv_kernel, qk_gain, None)
    mine, recv = reduce_pieces(*gradients(keys, values, weights1, False))
    moment, state, narrow = update(step_size, mine, recv, state, moment)
    weights2 = assemble(gather_pieces(narrow))
    queries0, queries1 = prepare_queries(q, qtails, conv_kernel, qk_gain)
    out = apply_fast(queries0, weights1, 0, None)
    return apply_fast(queries1, weights2, 1, out)


def solution(mesh):
    in_specs = (
        P(None, None, ("seq", "wide"), None),
        P(),
        P(None, "wide", None),
        P(None, "wide", None, None),
        P("wide"),
    )
    out_specs = P(None, "seq", "wide")
    return jax.shard_map(local, mesh=mesh, in_specs=in_specs, out_specs=out_specs, check_vma=False)
```

```python
import jax
import jax.numpy as jnp
from jax import lax
from jax.experimental import pallas as pl
from jax.experimental.pallas import tpu as pltpu
from jax.sharding import PartitionSpec as P


HEAD = 512
GROUPS = 2
KW = 4
EPS = 1e-06
BETA = 0.6
ROWS = 1024
CHUNK = 256
BLOCKS = ROWS // CHUNK
LEAD = CHUNK // 64
BF = jnp.bfloat16
F32 = jnp.float32


def vmem():
    return pl.BlockSpec(memory_space=pltpu.VMEM)


def anywhere():
    return pl.BlockSpec(memory_space=pl.ANY)


def call(body, outs, ins, scratch=(), flops=0, nbytes=1 << 18, out_specs=None, limit=16, **more):
    return pl.pallas_call(
        body,
        out_shape=outs,
        in_specs=ins,
        out_specs=jax.tree.map(lambda _: vmem(), outs) if out_specs is None else out_specs,
        scratch_shapes=list(scratch),
        cost_estimate=pl.CostEstimate(flops=flops, bytes_accessed=nbytes, transcendentals=0),
        compiler_params=pltpu.CompilerParams(vmem_limit_bytes=limit << 20),
        **more,
    )


def sds(shape, dtype):
    return jax.ShapeDtypeStruct(shape, dtype)


def sigmoid(x):
    return 0.5 * jnp.tanh(0.5 * x) + 0.5


def conv_silu(current, previous, taps):
    extended = jnp.concatenate([previous, current], axis=0)
    total = taps[0:1] * current
    for j in range(1, KW):
        total = total + taps[j : j + 1] * pltpu.roll(extended, j, 0)[8:]
    return (total * sigmoid(total)).astype(BF)


def rms_scaled(act, gain):
    wide = act.astype(F32)
    scale = lax.rsqrt(jnp.mean(wide * wide, axis=-1, keepdims=True) + EPS)
    return (wide * scale * gain).astype(BF)


def nt(left, right):
    return lax.dot_general(left, right, (((1,), (1,)), ((), ())), preferred_element_type=F32)


def nn(left, right):
    return jnp.dot(left, right, preferred_element_type=F32)


def tn(left, right):
    return lax.dot_general(left, right, (((0,), (0,)), ((), ())), preferred_element_type=F32)


def own_taps(taps, stream):
    cols = pl.ds(pl.multiple_of(lax.axis_index("wide") * HEAD, HEAD), HEAD)
    return taps[stream, :, cols]


def edge_rows(tails, stream, group):
    def taken(at):
        return sum(part[stream, at].astype(F32) for part in tails)

    later = lax.axis_index("seq") > 0
    here = taken(group)
    before = jnp.zeros_like(here) if group == 0 else taken(group - 1)
    return jnp.where(later, here, before)


def conv_chunk(raw, stream, n, edge, taps):
    current = raw[stream, pl.ds(LEAD * n, LEAD)].reshape(CHUNK, HEAD).astype(F32)
    inner = raw[stream, jnp.maximum(LEAD * n - 1, 0), 48:64, :].astype(F32)[8:]
    return conv_silu(current, jnp.where(n == 0, edge, inner), taps)


def raw_copy(source, raw, sems, offset, stream, n):
    lead = pl.ds(LEAD * n, LEAD)
    return pltpu.make_async_copy(
        source.at[lead, offset + stream], raw.at[stream, lead], sems.at[stream, n]
    )


def raw_scratch(streams):
    return [pltpu.VMEM((streams, 16, 64, HEAD), BF), pltpu.SemaphoreType.DMA((streams, BLOCKS))]


def chunk_rows(n):
    return pl.ds(pl.multiple_of(n * CHUNK, CHUNK), CHUNK)


def hbm():
    return pl.BlockSpec(memory_space=pltpu.HBM)


def in_hbm(value):
    return pltpu.with_memory_space_constraint(value, pltpu.HBM)


def prepare(group, source, tails, taps, gain, start):
    first = start is not None

    def body(source, *rest):
        tails, (taps, gain, *rest) = rest[:4], rest[4:]
        if first:
            start, keys, values, narrow, raw, sems, wide, wide_sem = rest
        else:
            keys, values, raw, sems = rest
        for n in range(BLOCKS):
            for stream in range(2):
                raw_copy(source, raw, sems, 0, stream, n).start()
        if first:
            fetch = pltpu.make_async_copy(start, wide, wide_sem)
            fetch.start()
        key_taps, value_taps = own_taps(taps, 1), own_taps(taps, 2)
        key_edge = edge_rows(tails, 1, group)
        value_edge = edge_rows(tails, 2, group)

        def step(n, carry):
            rows = chunk_rows(n)
            raw_copy(source, raw, sems, 0, 0, n).wait()
            raw_copy(source, raw, sems, 0, 1, n).wait()
            keys[rows, :] = rms_scaled(conv_chunk(raw, 0, n, key_edge, key_taps), gain[1])
            act = conv_chunk(raw, 1, n, value_edge, value_taps)
            values[rows, :] = (act.astype(F32) * (-1.0 / 16384)).astype(BF)
            return carry

        lax.fori_loop(0, BLOCKS, step, 0)
        if first:
            fetch.wait()
            narrow[...] = wide[...].astype(BF)

    rows = sds((ROWS, HEAD), BF)
    square = (3, HEAD, HEAD)
    outs = [rows, rows] + ([sds(square, BF)] if first else [])
    scratch = raw_scratch(2) + ([pltpu.VMEM(square, F32), pltpu.SemaphoreType.DMA(())] if first else [])
    ins = [in_hbm(source), *tails, taps, gain] + ([in_hbm(start)] if first else [])
    specs = [hbm()] + [vmem()] * 6 + ([hbm()] if first else [])
    return call(body, outs, specs, scratch, nbytes=8 << 20, limit=24)(*ins)


def prepare_queries(source, tails, taps, gain):
    def body(source, *rest):
        tails, (taps, gain, *rest) = rest[:4], rest[4:]
        raw, sems = rest[-2:]
        for group in range(GROUPS):
            for n in range(BLOCKS):
                raw_copy(source, raw, sems, 0, group, n).start()
        query_taps = own_taps(taps, 0)
        for group, queries in enumerate(rest[:GROUPS]):
            edge = edge_rows(tails, 0, group)

            def step(n, carry, group=group, queries=queries, edge=edge):
                raw_copy(source, raw, sems, 0, group, n).wait()
                act = conv_chunk(raw, group, n, edge, query_taps)
                queries[chunk_rows(n), :] = rms_scaled(act, gain[0])
                return carry

            lax.fori_loop(0, BLOCKS, step, 0)

    rows = sds((ROWS, HEAD), BF)
    return call(
        body, [rows, rows], [hbm()] + [vmem()] * 6, raw_scratch(GROUPS), nbytes=8 << 20
    )(in_hbm(source), *tails, taps, gain)


def gradients(keys, values, weights, plain):
    def body(keys, values, weights, keep, send, hs, gs, us):
        core = lax.axis_index("seq") & 1
        wg, wu, wd = (weights[m].astype(BF) for m in range(3))

        def step(n, carry):
            rows = chunk_rows(n)
            k = keys[rows, :]
            v = values[rows, :]
            if plain:
                a, b, back = nn(k, wg), nn(k, wu), nt(v, wd)
            else:
                a, b, back = nt(k, wg), nt(k, wu), nn(v, wd)
            sg = sigmoid(a)
            act = a * sg
            hs[rows, :] = (act * b).astype(BF)
            gs[rows, :] = (back * b * sg * (1.0 + a * (1.0 - sg))).astype(BF)
            us[rows, :] = (back * act).astype(BF)
            return carry

        lax.fori_loop(0, BLOCKS, step, 0)
        for half, out in ((1, send), (0, keep)):
            side = jnp.bitwise_xor(core, half)

            def block(n, carry, out=out, side=side):
                cols = pl.ds(pl.multiple_of(side * 256 + n * 128, 128), 128)
                for m, (left, right) in enumerate(((gs, keys), (us, keys), (values, hs))):
                    part = tn(left[:, cols], right[...]).astype(BF)
                    for q in range(2):
                        out[2 * n + q, m] = part[64 * q : 64 * q + 64]
                return carry

            lax.fori_loop(0, 2, block, 0)

    half = sds((4, 3, 64, HEAD), BF)
    return call(
        body,
        [half, half],
        [vmem()] * 3,
        [pltpu.VMEM((ROWS, HEAD), BF)] * 3,
        flops=6 * 2 * ROWS * HEAD * HEAD,
        nbytes=4 << 20,
        limit=24,
    )(keys, values, weights)


def pair_sum(keep, recv):
    def body(keep, recv, own, *sends):
        y = lax.axis_index("seq") >> 1 & 3
        own[...] = keep[y].astype(F32) + recv[y].astype(F32)
        for d, out in enumerate(sends):
            other = y + (d + 1) & 3
            out[...] = (keep[other].astype(F32) + recv[other].astype(F32)).astype(BF)

    block = (3, 64, HEAD)
    return call(body, [sds(block, F32)] + [sds(block, BF)] * 3, [vmem()] * 2)(keep, recv)


def ring_sum(own, parts):
    def body(own, one, two, three, out):
        out[...] = (own[...] + one[...].astype(F32) + two[...].astype(F32) + three[...].astype(F32)).astype(BF)

    return call(body, sds((3, 64, HEAD), BF), [vmem()] * 4)(own, *parts)


def update(scale, mine, recv, weights, moment):
    fresh = moment is None

    def body(scale, mine, recv, weights, *rest):
        grad = mine[...].astype(F32) + recv[...].astype(F32)
        if fresh:
            mom = grad
        else:
            mom = BETA * rest[0][...] + grad
        moment_out, weights_out, narrow = rest[-3:]
        norm = lax.rsqrt(jnp.mean(mom * mom, axis=-1, keepdims=True) + EPS)
        new = weights[...] - (scale[0] * HEAD ** (-0.5)) * (mom * norm)
        moment_out[...] = mom
        weights_out[...] = new
        narrow[...] = new.astype(BF)

    block = (3, 64, HEAD)
    ins = [scale, mine, recv, weights] + ([] if fresh else [moment])
    return call(
        body,
        [sds(block, F32), sds(block, F32), sds(block, BF)],
        [pl.BlockSpec(memory_space=pltpu.SMEM)] + [vmem()] * (len(ins) - 1),
    )(*ins)


def assemble(pieces):
    def body(*refs):
        out = refs[8]
        seq = lax.axis_index("seq")
        core, y = seq & 1, seq >> 1 & 3
        for k, piece in enumerate(refs[:8]):
            side = jnp.bitwise_xor(core, k // 4)
            spot = y + 4 - k % 4 & 3
            rows = pl.ds(pl.multiple_of(side * 256 + spot * 64, 64), 64)
            for m in range(3):
                out[m, rows, :] = piece[m]

    return call(body, sds((3, HEAD, HEAD), BF), [vmem()] * 8)(*pieces)


def apply_fast(queries, weights, group, earlier):
    def body(queries, weights, *rest):
        out, stage, sems = rest[-3:]

        def copy(n):
            rows = chunk_rows(n)
            return pltpu.make_async_copy(stage.at[rows], out.at[group, rows], sems.at[n])

        def step(n, carry):
            rows = chunk_rows(n)
            q = queries[rows, :]
            a = nt(q, weights[0])
            b = nt(q, weights[1])
            hidden = (a * sigmoid(a) * b).astype(BF)
            stage[rows, :] = nt(hidden, weights[2]).astype(BF)
            copy(n).start()
            return carry

        lax.fori_loop(0, BLOCKS, step, 0)
        for n in range(BLOCKS):
            copy(n).wait()

    more = [] if earlier is None else [earlier]
    return call(
        body,
        sds((GROUPS, ROWS, HEAD), BF),
        [vmem()] * 2 + [anywhere()] * len(more),
        [pltpu.VMEM((ROWS, HEAD), BF), pltpu.SemaphoreType.DMA((BLOCKS,))],
        flops=3 * 2 * ROWS * HEAD * HEAD,
        nbytes=4 << 20,
        out_specs=anywhere(),
        input_output_aliases={2: 0} if more else {},
    )(queries, weights, *more)


def seq_permute(value, target):
    return lax.ppermute(value, "seq", [(i, target(i)) for i in range(16)])


def core_swap(value):
    return seq_permute(value, lambda i: i ^ 1)


def z_swap(value):
    return seq_permute(value, lambda i: i ^ 8)


def y_shift(value, d):
    return seq_permute(value, lambda i: (i & 9) | (((i >> 1 & 3) + d & 3) << 1))


def regroup(qkv_proj, spots):
    def by_head(sources, dests):
        return [(pair_at(sources[0], spots, h * HEAD), dests[0].at[h]) for h in range(16)]

    (ready,) = move([qkv_proj], [sds((16, 2, 64, HEAD), BF)], (16, 2, 64, HEAD), by_head)
    return lax.all_to_all(ready, "wide", 0, 0, tiled=True)


def move(ins, outs, stages, moves):
    def body(*refs):
        sources, dests = refs[: len(ins)], refs[len(ins) : len(ins) + len(outs)]
        stage, sems_in, sems_out = refs[len(ins) + len(outs) :]
        jobs = moves(sources, dests)

        def pull(n):
            return pltpu.make_async_copy(jobs[n][0], stage.at[n], sems_in.at[n])

        def push(n):
            return pltpu.make_async_copy(stage.at[n], jobs[n][1], sems_out.at[n])

        for n in range(len(jobs)):
            pull(n).start()
        for n in range(len(jobs)):
            pull(n).wait()
            push(n).start()

        def settle(n, carry):
            pltpu.make_async_copy(stage.at[n], stage.at[n], sems_out.at[n]).wait()
            return carry

        lax.fori_loop(0, len(jobs), settle, 0)

    return call(
        body,
        outs,
        [hbm()] * len(ins),
        [pltpu.VMEM(stages, BF), pltpu.SemaphoreType.DMA(stages[:1]), pltpu.SemaphoreType.DMA(stages[:1])],
        nbytes=4 << 20,
        out_specs=jax.tree.map(lambda _: hbm(), outs),
        limit=60,
    )(*[in_hbm(value) for value in ins])


def wide_spot():
    wide = lax.axis_index("wide")
    return wide >> 2, wide & 3


def pair_at(source, spots, cols):
    (stream, group), (_, last) = spots
    if group == last:
        return source.at[pl.ds(stream, 2), group, :, pl.ds(cols, HEAD)]
    return source.at[stream, pl.ds(group, 2), :, pl.ds(cols, HEAD)]


def two_steps(qkv_proj, spots):
    block = sds((4, 2, 64, HEAD), BF)

    def by_x(sources, dests):
        x, _ = wide_spot()
        jobs = []
        for k in range(4):
            for z in range(4):
                cols = pl.multiple_of(((x + k & 3) * 4 + z) * HEAD, HEAD)
                jobs.append((pair_at(sources[0], spots, cols), dests[k].at[z]))
        return jobs

    def by_z(sources, dests):
        _, z = wide_spot()
        return [(sources[k].at[z + j & 3], dests[j].at[k]) for j in range(4) for k in range(4)]

    def by_source(sources, dests):
        x, z = wide_spot()
        return [
            (sources[j].at[k], dests[0].at[(x + 4 - k & 3) * 4 + (z + 4 - j & 3)])
            for j in range(4)
            for k in range(4)
        ]

    parts = move([qkv_proj], [block] * 4, (16, 2, 64, HEAD), by_x)
    parts = [parts[0]] + [wide_shift(parts[d], d, 0) for d in (1, 3, 2)]
    parts = [parts[0], parts[1], parts[3], parts[2]]
    parts = move(parts, [block] * 4, (16, 2, 64, HEAD), by_z)
    parts = [parts[0]] + [wide_shift(parts[d], 0, d) for d in (1, 3, 2)]
    parts = [parts[0], parts[1], parts[3], parts[2]]
    whole = move(parts, [sds((16, 2, 64, HEAD), BF)], (16, 2, 64, HEAD), by_source)
    return whole[0]


def wide_shift(value, dx, dz):
    pairs = [(w, ((w >> 2) + dx & 3) * 4 + ((w & 3) + dz & 3)) for w in range(16)]
    return lax.ppermute(value, "wide", pairs)


def tails_behind(qkv_proj):
    width = 4 * HEAD
    pieces = [qkv_proj[:, :, 56:64, x * width : x * width + width] for x in range(4)]
    x, _ = wide_spot()
    found = jnp.where(x == 3, pieces[3], jnp.zeros_like(pieces[3]))
    for d in range(3):
        found = found + lax.ppermute(pieces[d], "wide", [(15, 4 * d + 3)])
    parts = []
    for t in range(4):
        pairs = [
            (s * 16 + 4 * at + 3, (s + 1) % 16 * 16 + 4 * at + t) for s in range(16) for at in range(4)
        ]
        piece = found[..., t * HEAD : t * HEAD + HEAD]
        parts.append(lax.ppermute(piece, ("seq", "wide"), pairs))
    return parts


def reduce_pieces(keep, send):
    recv = core_swap(send)
    own, *sends = pair_sum(keep, recv)
    parts = [y_shift(s, d + 1) for d, s in enumerate(sends)]
    mine = ring_sum(own, parts)
    return mine, z_swap(mine)


def gather_pieces(narrow):
    pieces = [narrow] + [y_shift(narrow, d) for d in (1, 2, 3)]
    return pieces + [core_swap(p) for p in pieces]


def local(qkv_proj, conv_kernel, qk_gain, fast_init, step_size):
    return program(qkv_proj, conv_kernel, qk_gain, fast_init[:, 0], step_size)


def program(qkv_proj, conv_kernel, qk_gain, start, step_size):
    seq = lax.axis_index("seq")
    own_at = (seq & 1) * 256 + (seq >> 1 & 3) * 64
    state = jnp.swapaxes(lax.dynamic_slice_in_dim(start, own_at, 64, 2), 1, 2)

    kv0 = regroup(qkv_proj, ((1, 0), (2, 0)))
    tails = tails_behind(qkv_proj)
    kv1 = two_steps(qkv_proj, ((1, 1), (2, 1)))
    q = two_steps(qkv_proj, ((0, 0), (0, 1)))

    keys, values, narrow = prepare(0, kv0, tails, conv_kernel, qk_gain, start)
    keep, send = gradients(keys, values, narrow, True)
    mine, recv = reduce_pieces(keep, send)
    moment, state, narrow = update(step_size, mine, recv, state, None)
    weights1 = assemble(gather_pieces(narrow))
    keys, values = prepare(1, kv1, tails, conv_kernel, qk_gain, None)
    keep, send = gradients(keys, values, weights1, False)
    mine, recv = reduce_pieces(keep, send)
    moment, state, narrow = update(step_size, mine, recv, state, moment)
    weights2 = assemble(gather_pieces(narrow))
    queries0, queries1 = prepare_queries(q, tails, conv_kernel, qk_gain)
    out = apply_fast(queries0, weights1, 0, None)
    return apply_fast(queries1, weights2, 1, out)


def solution(mesh):
    in_specs = (
        P(None, None, ("seq", "wide"), None),
        P(),
        P(None, "wide", None),
        P(None, "wide", None, None),
        P("wide"),
    )
    out_specs = P(None, "seq", "wide")
    return jax.shard_map(local, mesh=mesh, in_specs=in_specs, out_specs=out_specs, check_vma=False)
```
